1024 devices in a mesh: seq: 16 (over x, core), dp: 64 (over y, z).
Axes of the slice: x: 8, y: 8, z: 8, core: 2. Of those that a mesh axis runs over, the one named last changes fastest.
Arguments:
- queries: bfloat16 [64, 2048, 4096], P('dp', 'seq'), may hold values from -6 to 6
- keys: bfloat16 [64, 2048, 512], P('dp', 'seq'), may hold values from -6 to 6
- values: bfloat16 [64, 2048, 512], P('dp', 'seq'), may hold values from -6 to 6
- grad_out: bfloat16 [64, 2048, 4096], P('dp', 'seq'), may hold values from -6 to 6
- features: bfloat16 [64, 2048, 4096], P('dp', 'seq'), may hold values from -100 to 100
- doc_lengths: int32 [64, 32], P('dp'), may hold values from 1 to 128, 2048 in all within a row
Outputs:
- key_grad: bfloat16 [64, 2048, 512], P('dp', 'seq')
- clipped_grad: float32 [4096, 512], P(('seq', 'dp'))
The draws below stay inside these ranges and needn't reach their ends.
Inputs may be any that keep to these rules, and one draw needn't show every extreme that they name: `doc_lengths`: each row sums to 2048; the longest document of every data group has exactly 128 tokens.
All inputs are finite; a program needn't handle non-finite values.
Results may differ from the reference program's by a relative error of at most 0.0058.
Values may be sent and summed in bfloat16 or wider, within the bound.
A program may use at most 32 MiB of HBM per device.

```python
import math
import jax
import jax.numpy as jnp
import numpy as np
from jax import lax

HD = 128
HQ = 32
KVH = 4
DW = 4096
DOC_MAX = 128
QBLK = 512
SEQ_LEN = 2048
NDOC = 32
N_SEQ = 16
N_DP = 64


def drawn_pair(key):
    base_seed = jax.random.fold_in(key, 11)
    query_seed = jax.random.fold_in(base_seed, 1)
    key_seed = jax.random.fold_in(base_seed, 2)
    query_drawn = jnp.clip(jax.random.normal(query_seed, (N_DP, SEQ_LEN, HQ * HD), jnp.float32), -4.0, 4.0)
    key_drawn = jnp.clip(jax.random.normal(key_seed, (N_DP, SEQ_LEN, KVH * HD), jnp.float32), -4.0, 4.0)
    return (query_drawn, key_drawn)


def value_pair(key):
    base_seed = jax.random.fold_in(key, 31)
    value_seed = jax.random.fold_in(base_seed, 1)
    noise_seed = jax.random.fold_in(base_seed, 2)
    value_drawn = jnp.clip(jax.random.normal(value_seed, (N_DP, SEQ_LEN, KVH * HD), jnp.float32), -4.0, 4.0)
    noise_drawn = jnp.clip(jax.random.normal(noise_seed, (N_DP, SEQ_LEN, HQ * HD), jnp.float32), -4.0, 4.0)
    value_four = value_drawn.reshape(N_DP, SEQ_LEN, KVH, HD)
    shared_heads = jnp.repeat(value_four, HQ // KVH, axis=2).reshape(N_DP, SEQ_LEN, HQ * HD)
    grad_drawn = 0.6 * shared_heads + 0.8 * noise_drawn
    return (value_drawn, grad_drawn)


def draw_queries(key, part):
    return drawn_pair(key)[0].astype(jnp.bfloat16)


def draw_keys(key, part):
    return drawn_pair(key)[1].astype(jnp.bfloat16)


def draw_values(key, part):
    return value_pair(key)[0].astype(jnp.bfloat16)


def draw_grad_out(key, part):
    return value_pair(key)[1].astype(jnp.bfloat16)


def draw_features(key, part):
    normal_seed = jax.random.fold_in(key, 21)
    column_seed = jax.random.fold_in(key, 22)
    row_seed = jax.random.fold_in(key, 23)
    offset_seed = jax.random.fold_in(key, 24)
    normal_part = jnp.clip(jax.random.normal(normal_seed, (N_DP, SEQ_LEN, DW), jnp.float32), -3.0, 3.0)
    column_rise = 3.0 ** (0.5 * jnp.arange(DW, dtype=jnp.float32) / DW)
    column_scale = 0.1 * 10.0 ** jax.random.uniform(column_seed, (DW,), jnp.float32) * column_rise
    row_scale = 10.0 ** jax.random.uniform(row_seed, (N_DP, SEQ_LEN, 1), jnp.float32)
    column_offset = 3.0 * (2 * jax.random.randint(offset_seed, (DW,), 0, 2) - 1).astype(jnp.float32)
    query_drawn = drawn_pair(key)[0]
    query_index = (jnp.arange(DW, dtype=jnp.int32) % (HQ * HD)).astype(jnp.int32)
    query_part = jnp.take(query_drawn, query_index, axis=2)
    mixed = normal_part * row_scale + 1.5 * query_part + column_offset
    return (mixed * column_scale).astype(jnp.bfloat16)


def length_profile(count, total, most, skew):
    weights = [(1 << 20) // math.isqrt(standing ** skew) + 1 for standing in range(2, count + 1)]
    rest, given = total - most - (count - 1), [1] * (count - 1)
    while rest > 0:
        free = [i for i in range(count - 1) if given[i] < most]
        whole, left = sum([weights[i] for i in free]), rest
        for i in free:
            addition = min(most - given[i], max(1, left * weights[i] // whole), rest)
            given[i] = given[i] + addition
            rest = rest - addition
    return np.array([most] + given)


def uneven_parts(own_key, amount, total, bound, lean):
    if amount == 2:
        one = jax.random.randint(own_key, (), max(1, total - bound), min(bound, total - 1) + 1)
        return jnp.stack([one, total - one])
    sizes = jnp.asarray(length_profile(amount, total, bound, lean), jnp.int32)
    pairs = (amount - 1) // 2
    donor, taker = sizes[1:1 + 2 * pairs:2], sizes[2:2 + 2 * pairs:2]
    margin = jnp.minimum(donor - 1, bound - taker)
    shifted = jax.random.randint(jax.random.fold_in(own_key, 1), (pairs,), 0, 1 << 20) % (margin + 1)
    sizes = sizes.at[1:1 + 2 * pairs:2].set(donor - shifted).at[2:2 + 2 * pairs:2].set(taker + shifted)
    return sizes[jax.random.permutation(jax.random.fold_in(own_key, 2), amount)]


def setup_inputs(seed: int = 0) -> dict:
    arg_keys = jax.random.split(jax.random.key(seed), 7)
    queries = draw_queries(jax.random.fold_in(arg_keys[6], 71), 0)
    keys = draw_keys(jax.random.fold_in(arg_keys[6], 71), 0)
    values = draw_values(jax.random.fold_in(arg_keys[6], 71), 0)
    grad_out = draw_grad_out(jax.random.fold_in(arg_keys[6], 71), 0)
    features = draw_features(jax.random.fold_in(arg_keys[6], 71), 0)
    doc_lengths = jax.vmap(lambda own: uneven_parts(own, NDOC, SEQ_LEN, DOC_MAX, 1))(jax.random.split(arg_keys[5], N_DP)).reshape((N_DP, NDOC)).astype(jnp.int32)
    return {"queries": queries, "keys": keys, "values": values, "grad_out": grad_out, "features": features, "doc_lengths": doc_lengths}


NEG_FILL = -1e+30

def doc_index(lengths, positions):
    doc_ends = jnp.cumsum(lengths, dtype=jnp.int32)
    located = lax.optimization_barrier(jnp.sum((doc_ends[None, :] <= positions[:, None]).astype(jnp.int32), axis=1))
    return jnp.where(positions < 0, -1, located).astype(jnp.int32)

def group_keys(group_pair):
    queries, keys, values, grad_out, lengths = group_pair
    slab_len = queries.shape[0]
    group_size = HQ // KVH
    sharers = N_SEQ // KVH
    local_heads = HQ // N_SEQ
    score_scale = 1.0 / math.sqrt(HD)
    block_width = QBLK + DOC_MAX
    query_four = queries.reshape(slab_len, KVH, group_size, HD).astype(jnp.float32)
    grad_four = grad_out.reshape(slab_len, KVH, group_size, HD).astype(jnp.float32)
    key_pad = jnp.concatenate([jnp.zeros((DOC_MAX, KVH, HD), jnp.float32), keys.reshape(slab_len, KVH, HD).astype(jnp.float32)], axis=0)
    value_pad = jnp.concatenate([jnp.zeros((DOC_MAX, KVH, HD), jnp.float32), values.reshape(slab_len, KVH, HD).astype(jnp.float32)], axis=0)

    def one_block(block_index, key_total):
        row_start = (block_index * QBLK).astype(jnp.int32)
        query_rows = lax.dynamic_slice_in_dim(query_four, row_start, QBLK, 0)
        grad_rows = lax.dynamic_slice_in_dim(grad_four, row_start, QBLK, 0)
        key_window = lax.dynamic_slice_in_dim(key_pad, row_start, block_width, 0)
        value_window = lax.dynamic_slice_in_dim(value_pad, row_start, block_width, 0)
        query_pos = row_start + jnp.arange(QBLK, dtype=jnp.int32)
        key_pos = row_start - DOC_MAX + jnp.arange(block_width, dtype=jnp.int32)
        query_doc = doc_index(lengths, query_pos)
        key_doc = doc_index(lengths, key_pos)
        visible = (query_doc[:, None] == key_doc[None, :]) & (key_pos[None, :] <= query_pos[:, None])
        scores = jnp.einsum('qrgd,krd->rgqk', query_rows, key_window, precision=lax.Precision.HIGHEST) * score_scale
        scores = jnp.where(visible[None, None], scores, NEG_FILL)
        row_peak = lax.optimization_barrier(jnp.max(scores, axis=3, keepdims=True))
        exponent = jnp.exp(scores - row_peak)
        attention = exponent / lax.optimization_barrier(jnp.sum(exponent, axis=3, keepdims=True))
        grad_weights = jnp.einsum('qrgd,krd->rgqk', grad_rows, value_window, precision=lax.Precision.HIGHEST)
        row_delta = lax.optimization_barrier(jnp.sum(attention * grad_weights, axis=3, keepdims=True))
        grad_scores = (attention * (grad_weights - row_delta) * score_scale).astype(jnp.bfloat16)
        grad_scores = lax.optimization_barrier(grad_scores).astype(jnp.float32)
        contribution = jnp.einsum('rgqk,qrgd->krgd', grad_scores, query_rows, precision=lax.Precision.HIGHEST)
        current = lax.dynamic_slice_in_dim(key_total, row_start, block_width, 0)
        return lax.dynamic_update_slice_in_dim(key_total, current + contribution, row_start, 0)
    key_total = lax.fori_loop(0, slab_len // QBLK, one_block, jnp.zeros((DOC_MAX + slab_len, KVH, group_size, HD), jnp.float32))
    device_parts = key_total[DOC_MAX:].reshape(slab_len, KVH, sharers, local_heads, HD).sum(axis=3)
    device_parts = lax.optimization_barrier(device_parts.astype(jnp.bfloat16)).astype(jnp.float32)
    return lax.optimization_barrier(jnp.sum(device_parts, axis=2)).reshape(slab_len, KVH * HD).astype(jnp.bfloat16)

def reference(queries, keys, values, grad_out, features, doc_lengths):
    key_grad = lax.map(group_keys, (queries, keys, values, grad_out, doc_lengths))

    def add_group(running, group_pair):
        group_features, group_grads = group_pair
        return (running + jnp.dot(group_features.T, group_grads, preferred_element_type=jnp.float32), None)
    weight_grad, unused = lax.scan(add_group, jnp.zeros((DW, KVH * HD), jnp.float32), (features, key_grad))
    root_mean = jnp.sqrt(jnp.mean(weight_grad * weight_grad) + 1e-06)
    clipped_grad = weight_grad * jnp.minimum(1.0, 1.0 / root_mean)
    return (key_grad, clipped_grad)
```

```python
import functools
import math

import jax
import jax.numpy as jnp
from jax import lax
from jax.experimental import pallas as pl
from jax.experimental.pallas import tpu as pltpu
from jax.sharding import PartitionSpec as P

HD = 128
KVH = 4
NEG_FILL = -1e30
MESH = pl.DeviceIdType.MESH
Z_CHIPS = 8
SUBS = 2


def kernel(
    dims, q_ref, k_ref, v_ref, do_ref, f_ref, len_ref, kg_ref, w_ref,
    k_prev, v_prev, grad_cols, key_own, back_send, back_recv,
    feat_cols, feat_send, pair_grad, weight, ring_send, ring_recv,
    mid_send, mid_recv, last_send, last_recv, sq_send, sq_recv,
    halo_sems, feat_sems, back_sems, pair_sems, ring_sems, mid_sems, last_sems, sq_sems,
):
    nx, ny, nz, rows, entry_count = dims
    tok = q_ref.shape[0]
    width = k_ref.shape[1]
    heads = q_ref.shape[1] // width
    half = width // 2
    sub = half // SUBS
    score_scale = 1.0 / math.sqrt(HD)

    seq, dp = lax.axis_index("seq"), lax.axis_index("dp")
    x, core = seq // 2, seq % 2
    y, z = dp // nz, dp % nz
    count = nx * 2
    right = (lax.rem(seq + 1, count), dp)
    left = (lax.rem(seq + count - 1, count), dp)
    partner = (x * 2 + 1 - core, dp)

    def at_x(step):
        return (lax.rem(x + step, nx) * 2 + core, dp)

    def at_y(step):
        return (seq, lax.rem(y + step, ny) * nz + z)

    def at_z(step):
        return (seq, y * nz + lax.rem(z + step, nz))

    barrier = pltpu.get_barrier_semaphore()
    pl.semaphore_signal(barrier, inc=1, device_id=left, device_id_type=MESH)
    pl.semaphore_signal(barrier, inc=1, device_id=right, device_id_type=MESH)
    for where_to, size in ((at_x, nx), (at_y, ny), (at_z, nz)):
        def greet(step, carry, where_to=where_to):
            pl.semaphore_signal(barrier, inc=1, device_id=where_to(step), device_id_type=MESH)
            return carry
        lax.fori_loop(1, size, greet, 0)

    def turn(block, carry):
        here = pl.multiple_of((block * 2 + core) * feat_cols.shape[1], 128)
        there = pl.multiple_of((block * 2 + 1 - core) * feat_cols.shape[1], 128)
        feat_cols[block, :, 0:tok] = f_ref[:, pl.ds(here, feat_cols.shape[1])].T
        feat_send[block] = f_ref[:, pl.ds(there, feat_cols.shape[1])].T
        return carry

    lax.fori_loop(0, nx, turn, 0)
    pl.semaphore_wait(barrier, 2 + (nx - 1) + (ny - 1) + (nz - 1))

    def remote(src, dst, sems, place, target):
        return pltpu.make_async_remote_copy(
            src_ref=src, dst_ref=dst, send_sem=sems.at[(0,) + place], recv_sem=sems.at[(1,) + place],
            device_id=target, device_id_type=MESH,
        )

    key_copy = remote(k_ref, k_prev, halo_sems, (0,), right)
    value_copy = remote(v_ref, v_prev, halo_sems, (1,), right)
    feat_copy = remote(feat_send, feat_cols.at[:, :, pl.ds(tok, tok)], feat_sems, (0,), partner)
    key_copy.start()
    value_copy.start()
    feat_copy.start()

    query_pos = seq * tok + lax.broadcasted_iota(jnp.int32, (1, tok), 1)
    key_pos = (seq - 1) * tok + lax.broadcasted_iota(jnp.int32, (2 * tok, tok), 0)

    def doc_start(doc, carry):
        total, start = carry
        total = total + len_ref[0, doc]
        return total, jnp.where(query_pos >= total, total, start)

    first_key = lax.fori_loop(0, len_ref.shape[1], doc_start, (jnp.int32(0), jnp.zeros((1, tok), jnp.int32)))[1]
    visible = (key_pos >= first_key) & (key_pos <= query_pos)

    key_copy.wait_recv()
    value_copy.wait_recv()

    def back_copy(group):
        return remote(back_send.at[group], back_recv.at[group], back_sems, (group,), left)

    def one_group(group, carry):
        cols = pl.ds(pl.multiple_of(group * HD, HD), HD)
        keys = jnp.concatenate([k_prev[:, cols], k_ref[:, cols]], axis=0)
        values = jnp.concatenate([v_prev[:, cols], v_ref[:, cols]], axis=0)
        queries = []
        for head in range(heads):
            at = pl.ds(pl.multiple_of((group * heads + head) * HD, HD), HD)
            query = q_ref[:, at]
            queries.append(query)
            scores = lax.dot_general(
                keys, query, (((1,), (1,)), ((), ())), preferred_element_type=jnp.float32
            ) * score_scale
            grad_weights = lax.dot_general(
                values, do_ref[:, at], (((1,), (1,)), ((), ())), preferred_element_type=jnp.float32
            )
            scores = jnp.where(visible, scores, NEG_FILL)
            exponent = jnp.exp(scores - jnp.max(scores, axis=0, keepdims=True))
            attention = exponent * (1.0 / jnp.sum(exponent, axis=0, keepdims=True))
            row_delta = jnp.sum(attention * grad_weights, axis=0, keepdims=True)
            grad_cols[:, head * HD:(head + 1) * HD] = (
                attention * (grad_weights - row_delta) * score_scale
            ).astype(jnp.bfloat16)
        key_part = jnp.dot(
            grad_cols[...], jnp.concatenate(queries, axis=0), preferred_element_type=jnp.float32
        )
        back_send[group] = key_part[:tok].astype(jnp.bfloat16)
        key_own[:, cols] = key_part[tok:]
        back_copy(group).start()
        return carry

    lax.fori_loop(0, KVH, one_group, 0)

    def add_back(group, carry):
        cols = pl.ds(pl.multiple_of(group * HD, HD), HD)
        back_copy(group).wait()
        done = (key_own[:, cols] + back_recv[group].astype(jnp.float32)).astype(jnp.bfloat16)
        kg_ref[:, cols] = done
        pair_grad[0:tok, cols] = done
        return carry

    lax.fori_loop(0, KVH, add_back, 0)
    pair_copy = remote(
        pair_grad.at[pl.ds(0, tok)], pair_grad.at[pl.ds(tok, tok)], pair_sems, (0,), partner
    )
    pair_copy.start()
    key_copy.wait_send()
    value_copy.wait_send()
    feat_copy.wait()
    pair_copy.wait()

    def multiply(block, carry):
        weight[block] = jnp.dot(
            feat_cols[block], pair_grad[...], preferred_element_type=jnp.float32
        ).reshape(weight.shape[1:])
        return carry

    lax.fori_loop(0, nx, multiply, 0)

    sides = (
        (0, nx, at_x, lambda step, cols: weight[lax.rem(x + step + nx, nx), :, :, cols]),
        (1, ny, at_y, lambda step, cols: weight[:, lax.rem(y + step + ny, ny), :, cols]),
    )

    others = (pl.ds(0, ny), pl.ds(0, nx))

    def ring_copy(side, way, piece, step, where_to, size):
        target = where_to(size - 1) if way == 0 else where_to(1)
        place = (side, way, piece, step, others[side])
        return remote(ring_send.at[place], ring_recv.at[place], ring_sems, place[:4], target)

    def reach(way, size):
        return size // 2 if way == 0 else (size - 1) // 2

    def columns(side, piece):
        return pl.ds(side * half + piece * sub, sub)

    most = max(nx, ny) // 2
    for step in range(most):
        for piece in range(SUBS):
            for way in range(2):
                for side, size, where_to, own in sides:
                    far = reach(way, size)
                    if step >= far:
                        continue
                    away = (step - far) if way == 0 else (far - step)
                    term = own(away, columns(side, piece))
                    if step > 0:
                        ring_copy(side, way, piece, step - 1, where_to, size).wait_recv()
                        term = term + ring_recv[side, way, piece, step - 1, others[side]].astype(jnp.float32)
                    ring_send[side, way, piece, step, others[side]] = term.astype(jnp.bfloat16)
                    ring_copy(side, way, piece, step, where_to, size).start()

    def mid_copy(side, step):
        where_to = at_y if side == 0 else at_x
        size = ny if side == 0 else nx
        index = lax.rem((y if side == 0 else x) + step, size)
        return remote(
            mid_send.at[side, index], mid_recv.at[side, step], mid_sems, (side, step), where_to(step)
        )

    sums = []
    for side, size, where_to, own in sides:
        pieces = []
        for piece in range(SUBS):
            term = own(0, columns(side, piece))
            for way in range(2):
                far = reach(way, size)
                if far:
                    ring_copy(side, way, piece, far - 1, where_to, size).wait_recv()
                    term = term + ring_recv[side, way, piece, far - 1, others[side]].astype(jnp.float32)
            pieces.append(term)
        whole = jnp.concatenate(pieces, axis=2)
        mid_send[side, others[side]] = whole.astype(jnp.bfloat16)
        other = ny if side == 0 else nx
        def send_mid(step, carry, side=side):
            mid_copy(side, step).start()
            return carry
        lax.fori_loop(1, other, send_mid, 0)
    for side, size, where_to, own in sides:
        other = ny if side == 0 else nx
        def add_mid(step, carry, side=side):
            mid_copy(side, step).wait_recv()
            return carry + mid_recv[side, step].astype(jnp.float32)
        mine = mid_send[side, y if side == 0 else x].astype(jnp.float32)
        sums.append(lax.fori_loop(1, other, add_mid, mine))
    block = jnp.concatenate(sums, axis=1)

    for index in range(nz):
        last_send[index] = block[index * rows:(index + 1) * rows]

    def last_copy(step):
        return remote(
            last_send.at[lax.rem(z + step, nz)], last_recv.at[step], last_sems, (step,), at_z(step)
        )

    def send_last(step, carry):
        last_copy(step).start()
        return carry

    def add_last(step, carry):
        last_copy(step).wait_recv()
        return carry + last_recv[step]

    lax.fori_loop(1, nz, send_last, 0)
    own_rows = lax.fori_loop(1, nz, add_last, last_send[z])

    squares = jnp.sum(own_rows * own_rows, axis=0, keepdims=True)
    squares = jnp.broadcast_to(
        jnp.sum(squares.reshape(1, width // HD, HD), axis=1), (8, HD)
    )
    axes = ((at_z, nz), (at_y, ny), (at_x, nx), (lambda step: partner, 2))
    for stage, (where_to, size) in enumerate(axes):
        sq_send[stage] = squares
        def sq_copy(step, stage=stage, where_to=where_to):
            return remote(sq_send.at[stage], sq_recv.at[stage, step], sq_sems, (stage, step), where_to(step))
        def send_sq(step, carry):
            sq_copy(step).start()
            return carry
        def add_sq(step, carry, stage=stage):
            sq_copy(step).wait_recv()
            return carry + sq_recv[stage, step]
        lax.fori_loop(1, size, send_sq, 0)
        squares = lax.fori_loop(1, size, add_sq, squares)
    total = jnp.sum(squares[0:1], axis=1, keepdims=True)
    root_mean = jnp.sqrt(total / entry_count + 1e-06)
    w_ref[...] = own_rows * jnp.minimum(1.0, 1.0 / root_mean)

    for step in range(most):
        for piece in range(SUBS):
            for way in range(2):
                for side, size, where_to, own in sides:
                    if step < reach(way, size):
                        ring_copy(side, way, piece, step, where_to, size).wait_send()
    for side in range(2):
        def end_mid(step, carry, side=side):
            mid_copy(side, step).wait_send()
            return carry
        lax.fori_loop(1, ny if side == 0 else nx, end_mid, 0)

    def end_last(step, carry):
        last_copy(step).wait_send()
        return carry

    lax.fori_loop(1, nz, end_last, 0)
    for stage, (where_to, size) in enumerate(axes):
        def end_sq(step, carry, stage=stage, where_to=where_to):
            remote(
                sq_send.at[stage], sq_recv.at[stage, step], sq_sems, (stage, step), where_to(step)
            ).wait_send()
            return carry
        lax.fori_loop(1, size, end_sq, 0)


def shards(sizes, queries, keys, values, grad_out, features, doc_lengths):
    seq_count, dp_count = sizes
    nz = min(Z_CHIPS, dp_count)
    nx, ny = seq_count // 2, dp_count // nz
    tok, wide = features.shape[1:]
    width = keys.shape[2]
    rows = wide // (seq_count * dp_count)
    low = nz * rows
    most = max(nx, ny)
    sub = width // 2 // SUBS
    dma = pltpu.SemaphoreType.DMA
    vmem = pl.BlockSpec(memory_space=pltpu.VMEM)
    bf16, f32 = jnp.bfloat16, jnp.float32
    key_grad, clipped = pl.pallas_call(
        functools.partial(kernel, (nx, ny, nz, rows, wide * width)),
        out_shape=(
            jax.ShapeDtypeStruct((tok, width), bf16),
            jax.ShapeDtypeStruct((rows, width), f32),
        ),
        in_specs=[vmem] * 5 + [pl.BlockSpec(memory_space=pltpu.SMEM)],
        out_specs=(vmem, vmem),
        scratch_shapes=[
            pltpu.VMEM((tok, width), bf16),
            pltpu.VMEM((tok, width), bf16),
            pltpu.VMEM((2 * tok, queries.shape[2] // KVH), bf16),
            pltpu.VMEM((tok, width), f32),
            pltpu.VMEM((KVH, tok, HD), bf16),
            pltpu.VMEM((KVH, tok, HD), bf16),
            pltpu.VMEM((nx, ny * low, 2 * tok), bf16),
            pltpu.VMEM((nx, ny * low, tok), bf16),
            pltpu.VMEM((2 * tok, width), bf16),
            pltpu.VMEM((nx, ny, low, width), f32),
            pltpu.VMEM((2, 2, SUBS, most // 2, most, low, sub), bf16),
            pltpu.VMEM((2, 2, SUBS, most // 2, most, low, sub), bf16),
            pltpu.VMEM((2, most, low, width // 2), bf16),
            pltpu.VMEM((2, most, low, width // 2), bf16),
            pltpu.VMEM((nz, rows, width), f32),
            pltpu.VMEM((nz, rows, width), f32),
            pltpu.VMEM((4, 8, HD), f32),
            pltpu.VMEM((4, max(most, nz), 8, HD), f32),
            dma((2, 2)),
            dma((2, 1)),
            dma((2, KVH)),
            dma((2, 1)),
            dma((2, 2, 2, SUBS, most // 2)),
            dma((2, 2, most)),
            dma((2, nz)),
            dma((2, 4, max(most, nz))),
        ],
        compiler_params=pltpu.CompilerParams(
            collective_id=0, has_side_effects=True, vmem_limit_bytes=48 << 20
        ),
    )(queries[0], keys[0], values[0], grad_out[0], features[0], doc_lengths)
    return key_grad[None], clipped


def solution(mesh):
    in_specs = (
        P("dp", "seq", None),
        P("dp", "seq", None),
        P("dp", "seq", None),
        P("dp", "seq", None),
        P("dp", "seq", None),
        P("dp", None),
    )
    out_specs = (P("dp", "seq", None), P(("seq", "dp"), None))
    return jax.shard_map(
        functools.partial(shards, (mesh.shape["seq"], mesh.shape["dp"])),
        mesh=mesh, in_specs=in_specs, out_specs=out_specs, check_vma=False,
    )
```

```python
import functools
import math

import jax
import jax.numpy as jnp
from jax import lax
from jax.experimental import pallas as pl
from jax.experimental.pallas import tpu as pltpu
from jax.sharding import PartitionSpec as P

HD = 128
KVH = 4
NEG_FILL = -1e30
MESH = pl.DeviceIdType.MESH
Z_CHIPS = 8
PARTS = 2

def kernel(
    dims, q_hbm, k_hbm, v_hbm, do_hbm, f_hbm, len_ref, kg_ref, w_ref,
    q_ref, k_ref, v_ref, do_ref, f_ref,
    k_prev, v_prev, grad_cols, key_own, back_send, back_recv,
    feat_cols, feat_send, pair_grad, weight, ring_send, ring_recv,
    mid_send, mid_recv, last_send, last_recv, sq_send, sq_recv,
    load_sems, halo_sems, feat_sems, back_sems, pair_sems, ring_sems, mid_sems, last_sems, sq_sems,
):
    nx, ny, nz, rows, entry_count = dims
    tok = q_ref.shape[0]
    width = k_ref.shape[1]
    heads = q_ref.shape[1] // width
    score_scale = 1.0 / math.sqrt(HD)
    f32, bf16 = jnp.float32, jnp.bfloat16

    seq, dp = lax.axis_index("seq"), lax.axis_index("dp")
    x, core = seq // 2, seq % 2
    y, z = dp // nz, dp % nz
    count = nx * 2
    left = (lax.rem(seq + count - 1, count), dp)
    partner = (x * 2 + 1 - core, dp)

    def at_seq(step):
        return (lax.rem(seq + step, count), dp)

    def at_x(step):
        return (lax.rem(x + step, nx) * 2 + core, dp)

    def at_y(step):
        return (seq, lax.rem(y + step, ny) * nz + z)

    def at_z(step):
        return (seq, y * nz + lax.rem(z + step, nz))

    barrier = pltpu.get_barrier_semaphore()
    for where_to, size in ((at_seq, count), (at_y, ny), (at_z, nz)):
        def greet(step, carry, where_to=where_to):
            pl.semaphore_signal(barrier, inc=1, device_id=where_to(step), device_id_type=MESH)
            return carry
        lax.fori_loop(1, size, greet, 0)

    pairs = ((k_hbm, k_ref), (v_hbm, v_ref), (f_hbm, f_ref), (q_hbm, q_ref), (do_hbm, do_ref))
    loads = [pltpu.make_async_copy(src, dst, load_sems.at[i]) for i, (src, dst) in enumerate(pairs)]
    for load in loads:
        load.start()

    def remote(src, dst, sems, place, target):
        return pltpu.make_async_remote_copy(
            src_ref=src, dst_ref=dst, send_sem=sems.at[(0,) + place], recv_sem=sems.at[(1,) + place],
            device_id=target, device_id_type=MESH,
        )

    def group_cols(group):
        return pl.ds(group * HD, HD)

    def halo_copies(group):
        cols = group_cols(group)
        return (
            remote(k_ref.at[:, cols], k_prev.at[:, cols], halo_sems, (0, group), at_seq(1)),
            remote(v_ref.at[:, cols], v_prev.at[:, cols], halo_sems, (1, group), at_seq(1)),
        )

    feat_copy = remote(feat_send, feat_cols.at[:, :, pl.ds(tok, tok)], feat_sems, (0,), partner)

    loads[0].wait()
    loads[1].wait()
    pl.semaphore_wait(barrier, (count - 1) + (ny - 1) + (nz - 1))
    for group in range(KVH):
        for copy in halo_copies(group):
            copy.start()

    query_pos = seq * tok + lax.broadcasted_iota(jnp.int32, (1, tok), 1)
    key_pos = (seq - 1) * tok + lax.broadcasted_iota(jnp.int32, (2 * tok, tok), 0)

    def doc_start(doc, carry):
        total, start = carry
        total = total + len_ref[0, doc]
        return total, jnp.where(query_pos >= total, total, start)

    first_key = lax.fori_loop(0, len_ref.shape[1], doc_start, (jnp.int32(0), jnp.zeros((1, tok), jnp.int32)))[1]
    visible = (key_pos >= first_key) & (key_pos <= query_pos)

    loads[2].wait()
    span = feat_cols.shape[1]

    def turn(block, carry):
        here = pl.multiple_of((block * 2 + core) * span, 128)
        there = pl.multiple_of((block * 2 + 1 - core) * span, 128)
        feat_send[block] = f_ref[:, pl.ds(there, span)].T
        feat_cols[block, :, 0:tok] = f_ref[:, pl.ds(here, span)].T
        return carry

    lax.fori_loop(0, nx, turn, 0)
    feat_copy.start()
    loads[3].wait()
    loads[4].wait()

    def back_copy(group):
        return remote(back_send.at[group], back_recv.at[group], back_sems, (group,), left)

    def attend(group):
        cols = group_cols(group)
        for copy in halo_copies(group):
            copy.wait_recv()
        keys = jnp.concatenate([k_prev[:, cols], k_ref[:, cols]], axis=0)
        values = jnp.concatenate([v_prev[:, cols], v_ref[:, cols]], axis=0)
        queries = []
        for head in range(heads):
            at = pl.ds((group * heads + head) * HD, HD)
            query = q_ref[:, at]
            queries.append(query)
            scores = lax.dot_general(
                keys, query, (((1,), (1,)), ((), ())), preferred_element_type=f32
            ) * score_scale
            grad_weights = lax.dot_general(
                values, do_ref[:, at], (((1,), (1,)), ((), ())), preferred_element_type=f32
            )
            scores = jnp.where(visible, scores, NEG_FILL)
            exponent = jnp.exp(scores - jnp.max(scores, axis=0, keepdims=True))
            attention = exponent * (1.0 / jnp.sum(exponent, axis=0, keepdims=True))
            row_delta = jnp.sum(attention * grad_weights, axis=0, keepdims=True)
            grad_cols[:, head * HD:(head + 1) * HD] = (
                attention * (grad_weights - row_delta) * score_scale
            ).astype(bf16)
        key_part = jnp.dot(
            grad_cols[...], jnp.concatenate(queries, axis=0), preferred_element_type=f32
        )
        back_send[group] = key_part[:tok].astype(bf16)
        back_copy(group).start()
        key_own[:, cols] = key_part[tok:]

    def pair_copy(group):
        cols = group_cols(group)
        return remote(
            pair_grad.at[pl.ds(0, tok), cols], pair_grad.at[pl.ds(tok, tok), cols],
            pair_sems, (group,), partner,
        )

    def add_back(group):
        cols = group_cols(group)
        back_copy(group).wait_recv()
        done = (key_own[:, cols] + back_recv[group].astype(f32)).astype(bf16)
        pair_grad[0:tok, cols] = done
        pair_copy(group).start()
        kg_ref[:, cols] = done

    def multiply(group):
        pair_copy(group).wait_recv()
        grads = pair_grad[:, group_cols(group)]

        def one_block(block, carry):
            weight[group, block] = jnp.dot(
                feat_cols[block], grads, preferred_element_type=f32
            ).reshape(weight.shape[2:])
            return carry

        lax.fori_loop(0, nx, one_block, 0)

    sides = (
        (nx, ny, at_x, at_y, x, y),
        (ny, nx, at_y, at_x, y, x),
    )

    def parts(group):
        other = sides[group % 2][1]
        cut = PARTS if other % PARTS == 0 else 1
        return [(part, pl.ds(part * (other // cut), other // cut)) for part in range(cut)]

    def own_term(group, away, some):
        size, mine = sides[group % 2][0], sides[group % 2][4]
        place = lax.rem(mine + away + size, size)
        return weight[group, place, some] if group % 2 == 0 else weight[group, some, place]

    def reach(group, way):
        size = sides[group % 2][0]
        return size // 2 if way == 0 else (size - 1) // 2

    def ring_copy(group, way, part, some, step):
        size, _, where_to = sides[group % 2][:3]
        place = (group, way, step, some)
        return remote(
            ring_send.at[place], ring_recv.at[place], ring_sems, (group, way, step, part),
            where_to(size - 1) if way == 0 else where_to(1),
        )

    def ring_step(group, step):
        for part, some in parts(group):
            for way in range(2):
                far = reach(group, way)
                if step >= far:
                    continue
                term = own_term(group, (step - far) if way == 0 else (far - step), some)
                if step > 0:
                    ring_copy(group, way, part, some, step - 1).wait_recv()
                    term = term + ring_recv[group, way, step - 1, some].astype(f32)
                ring_send[group, way, step, some] = term.astype(bf16)
                ring_copy(group, way, part, some, step).start()

    def mid_copy(group, step):
        _, other, _, where_to, _, mine = sides[group % 2]
        return remote(
            mid_send.at[group, lax.rem(mine + step, other)], mid_recv.at[group, step],
            mid_sems, (group, step), where_to(step),
        )

    def ring_end(group):
        for part, some in parts(group):
            term = own_term(group, 0, some)
            for way in range(2):
                far = reach(group, way)
                if far:
                    ring_copy(group, way, part, some, far - 1).wait_recv()
                    term = term + ring_recv[group, way, far - 1, some].astype(f32)
            mid_send[group, some] = term.astype(bf16)

        def send_mid(step, carry):
            mid_copy(group, step).start()
            return carry

        lax.fori_loop(1, sides[group % 2][1], send_mid, 0)

    for group in range(KVH):
        attend(group)
        if group >= 1:
            add_back(group - 1)
        if group == 1:
            feat_copy.wait_recv()
        if group >= 2:
            multiply(group - 2)
            ring_step(group - 2, 0)
    ring_step(0, 1)
    add_back(KVH - 1)
    multiply(KVH - 2)
    ring_step(KVH - 2, 0)
    multiply(KVH - 1)
    ring_step(KVH - 1, 0)

    due = (6.8, 9.4, 11.3, 12.4)
    turns = []
    for group in range(KVH):
        last = max(reach(group, 0), reach(group, 1))
        for step in range(2 if group == 0 else 1, last + 1):
            turns.append((due[group] + 2.7 * step, group, step, step == last))
        if last == 0 or (group == 0 and last == 1):
            turns.append((due[group] + 2.7 * last, group, last, True))
    for _, group, step, end in sorted(turns):
        if end:
            ring_end(group)
        else:
            ring_step(group, step)

    sums = []
    for group in range(KVH):
        def add_mid(step, carry, group=group):
            mid_copy(group, step).wait_recv()
            return carry + mid_recv[group, step].astype(f32)
        mine = mid_send[group, sides[group % 2][5]].astype(f32)
        sums.append(lax.fori_loop(1, sides[group % 2][1], add_mid, mine))
    block = jnp.concatenate(sums, axis=1)

    for index in range(nz):
        last_send[index] = block[index * rows:(index + 1) * rows]

    def last_copy(step):
        return remote(
            last_send.at[lax.rem(z + step, nz)], last_recv.at[step], last_sems, (step,), at_z(step)
        )

    def send_last(step, carry):
        last_copy(step).start()
        return carry

    def add_last(step, carry):
        last_copy(step).wait_recv()
        return carry + last_recv[step]

    lax.fori_loop(1, nz, send_last, 0)
    own_rows = lax.fori_loop(1, nz, add_last, last_send[z])

    squares = jnp.sum(own_rows * own_rows, axis=0, keepdims=True)
    squares = jnp.broadcast_to(
        jnp.sum(squares.reshape(1, width // HD, HD), axis=1), (8, HD)
    )
    axes = ((at_z, nz), (at_y, ny), (at_seq, count))

    def sq_copy(stage, step):
        return remote(
            sq_send.at[stage], sq_recv.at[stage, step], sq_sems, (stage, step), axes[stage][0](step)
        )

    for stage, (_, size) in enumerate(axes):
        sq_send[stage] = squares
        def send_sq(step, carry, stage=stage):
            sq_copy(stage, step).start()
            return carry
        def add_sq(step, carry, stage=stage):
            sq_copy(stage, step).wait_recv()
            return carry + sq_recv[stage, step]
        lax.fori_loop(1, size, send_sq, 0)
        squares = lax.fori_loop(1, size, add_sq, squares)
    total = jnp.sum(squares[0:1], axis=1, keepdims=True)
    root_mean = jnp.sqrt(total / entry_count + 1e-06)
    w_ref[...] = own_rows * jnp.minimum(1.0, 1.0 / root_mean)

    feat_copy.wait_send()
    for group in range(KVH):
        for copy in halo_copies(group):
            copy.wait_send()
        back_copy(group).wait_send()
        pair_copy(group).wait_send()
        for part, some in parts(group):
            for way in range(2):
                for step in range(reach(group, way)):
                    ring_copy(group, way, part, some, step).wait_send()
        def end_mid(step, carry, group=group):
            mid_copy(group, step).wait_send()
            return carry
        lax.fori_loop(1, sides[group % 2][1], end_mid, 0)

    def end_last(step, carry):
        last_copy(step).wait_send()
        return carry

    lax.fori_loop(1, nz, end_last, 0)
    for stage, (_, size) in enumerate(axes):
        def end_sq(step, carry, stage=stage):
            sq_copy(stage, step).wait_send()
            return carry
        lax.fori_loop(1, size, end_sq, 0)


def shards(sizes, queries, keys, values, grad_out, features, doc_lengths):
    seq_count, dp_count = sizes
    nz = min(Z_CHIPS, dp_count)
    nx, ny = seq_count // 2, dp_count // nz
    tok, wide = features.shape[1:]
    width = keys.shape[2]
    rows = wide // (seq_count * dp_count)
    low = nz * rows
    most = max(nx, ny)
    dma = pltpu.SemaphoreType.DMA
    vmem = pl.BlockSpec(memory_space=pltpu.VMEM)
    bf16, f32 = jnp.bfloat16, jnp.float32
    key_grad, clipped = pl.pallas_call(
        functools.partial(kernel, (nx, ny, nz, rows, wide * width)),
        out_shape=(
            jax.ShapeDtypeStruct((tok, width), bf16),
            jax.ShapeDtypeStruct((rows, width), f32),
        ),
        in_specs=[pl.BlockSpec(memory_space=pltpu.HBM)] * 5 + [pl.BlockSpec(memory_space=pltpu.SMEM)],
        out_specs=(vmem, vmem),
        scratch_shapes=[
            pltpu.VMEM((tok, queries.shape[2]), bf16),
            pltpu.VMEM((tok, width), bf16),
            pltpu.VMEM((tok, width), bf16),
            pltpu.VMEM((tok, queries.shape[2]), bf16),
            pltpu.VMEM((tok, wide), bf16),
            pltpu.VMEM((tok, width), bf16),
            pltpu.VMEM((tok, width), bf16),
            pltpu.VMEM((2 * tok, queries.shape[2] // KVH), bf16),
            pltpu.VMEM((tok, width), f32),
            pltpu.VMEM((KVH, tok, HD), bf16),
            pltpu.VMEM((KVH, tok, HD), bf16),
            pltpu.VMEM((nx, ny * low, 2 * tok), bf16),
            pltpu.VMEM((nx, ny * low, tok), bf16),
            pltpu.VMEM((2 * tok, width), bf16),
            pltpu.VMEM((KVH, nx, ny, low, HD), f32),
            pltpu.VMEM((KVH, 2, most // 2, most, low, HD), bf16),
            pltpu.VMEM((KVH, 2, most // 2, most, low, HD), bf16),
            pltpu.VMEM((KVH, most, low, HD), bf16),
            pltpu.VMEM((KVH, most, low, HD), bf16),
            pltpu.VMEM((nz, rows, width), f32),
            pltpu.VMEM((nz, rows, width), f32),
            pltpu.VMEM((3, 8, HD), f32),
            pltpu.VMEM((3, max(seq_count, ny, nz), 8, HD), f32),
            dma((5,)),
            dma((2, 2, KVH)),
            dma((2, 1)),
            dma((2, KVH)),
            dma((2, KVH)),
            dma((2, KVH, 2, most // 2, PARTS)),
            dma((2, KVH, most)),
            dma((2, nz)),
            dma((2, 3, max(seq_count, ny, nz))),
        ],
        compiler_params=pltpu.CompilerParams(
            collective_id=0, has_side_effects=True, vmem_limit_bytes=60 << 20
        ),
    )(queries[0], keys[0], values[0], grad_out[0], features[0], doc_lengths)
    return key_grad[None], clipped


def solution(mesh):
    in_specs = (
        P("dp", "seq", None),
        P("dp", "seq", None),
        P("dp", "seq", None),
        P("dp", "seq", None),
        P("dp", "seq", None),
        P("dp", None),
    )
    out_specs = (P("dp", "seq", None), P(("seq", "dp"), None))
    return jax.shard_map(
        functools.partial(shards, (mesh.shape["seq"], mesh.shape["dp"])),
        mesh=mesh, in_specs=in_specs, out_specs=out_specs, check_vma=False,
    )
```
